32 devices in a mesh: segment: 4 (over z), seq: 8 (over y, x, core).
Axes of the slice: x: 2, y: 2, z: 4, core: 2. Of those that a mesh axis runs over, the one named last changes fastest.
Arguments:
- sequence: bfloat16 [256, 512, 256], P('seq', 'segment'), may hold values from -6 to 6
- first_factors: bfloat16 [4, 4, 256, 256], P('segment'), may hold values from -0.375 to 0.375
- second_factors: bfloat16 [4, 4, 256, 256], P('segment'), may hold values from -0.375 to 0.375
- kernels: bfloat16 [4, 2, 256, 256], P('segment', None, 'seq'), may hold values from -6 to 6
- gate_scale: float32 [4, 512], P('segment'), may hold values from -2 to 2
- gate_bias: float32 [4, 512], P('segment'), may hold values from -1 to 1
Outputs:
- mixed: bfloat16 [256, 512, 256], P('seq', 'segment')
The draws below stay inside these ranges and needn't reach their ends.
All inputs are finite; a program needn't handle non-finite values.
Results may differ from the reference program's by a relative error of at most 0.024.
Values may be sent and summed in bfloat16 or wider, within the bound.
A program may use at most 64 MiB of HBM per device.

```python
import jax
import jax.numpy as jnp

RADIX = 256
D = 512
LAYERS = 4


def steps_of(key, shape, pieces, least, top_value):
    level, own = 1.0, jax.random.fold_in(key, 6)
    for position, blocks in pieces:
        steps = jnp.exp(jax.random.uniform(jax.random.fold_in(own, position), (blocks,), jnp.float32, least / len(pieces), top_value / len(pieces)))
        level = level * jnp.repeat(steps, shape[position] // blocks).reshape([-1 if axis == position else 1 for axis in range(len(shape))])
    return level


def gaussian(key, extent, width, most, pieces=(), dtype=jnp.bfloat16):
    values = width * jax.random.normal(key, extent, jnp.float32)
    if pieces:
        values = values * steps_of(key, extent, pieces, -0.22, 0.18)
    return jnp.clip(values, -most, most).astype(dtype)


def setup_inputs(seed: int = 0) -> dict:
    splits = jax.random.split(jax.random.key(seed), 7)
    return {
        "sequence": gaussian(splits[0], (RADIX, D, RADIX), 1.0, 6.0, ((0, 8), (1, 4))),
        "first_factors": gaussian(splits[1], (LAYERS, 4, RADIX, RADIX), RADIX ** -0.5, 0.375, ((0, 4),)),
        "second_factors": gaussian(splits[2], (LAYERS, 4, RADIX, RADIX), RADIX ** -0.5, 0.375, ((0, 4),)),
        "kernels": gaussian(splits[3], (LAYERS, 2, RADIX, RADIX), 1.0, 6.0, ((0, 4), (2, 8))),
        "gate_scale": jnp.clip(jax.random.uniform(splits[4], (LAYERS, D), jnp.float32, -2.0, 2.0) * steps_of(splits[4], (LAYERS, D), ((0, 4),), -0.4, 0.0), -2.0, 2.0),
        "gate_bias": jnp.clip(jax.random.uniform(splits[5], (LAYERS, D), jnp.float32, -1.0, 1.0) * steps_of(splits[5], (LAYERS, D), ((0, 4),), -0.4, 0.0), -1.0, 1.0),
    }


def monarch(values, first, second):
    mixed = jnp.einsum('pcq,kq->pck', values.astype(jnp.float32), first.astype(jnp.float32)).astype(jnp.bfloat16)
    return jnp.einsum('pck,jp->kcj', mixed.astype(jnp.float32), second.astype(jnp.float32))


def layer_apply(values, first, second, kernel_pair, scales, biases):
    kernel_one = kernel_pair[0].astype(jnp.float32)[:, None, :]
    kernel_two = kernel_pair[1].astype(jnp.float32)[:, None, :]
    widened = values.astype(jnp.float32)
    branch_one = (monarch(values, first[0], second[0]) * kernel_one).astype(jnp.bfloat16)
    gating = jax.nn.sigmoid(scales[None, :, None] * widened + biases[None, :, None])
    gated = (monarch(branch_one, first[1], second[1]) * gating).astype(jnp.bfloat16)
    branch_two = (monarch(gated, first[2], second[2]) * kernel_two).astype(jnp.bfloat16)
    return (widened + monarch(branch_two, first[3], second[3])).astype(jnp.bfloat16)


def reference(sequence, first_factors, second_factors, kernels, gate_scale, gate_bias):
    current = sequence
    for level in range(LAYERS):
        current = layer_apply(current, first_factors[level], second_factors[level], kernels[level], gate_scale[level], gate_bias[level])
    return current
```

```python
import jax
import jax.numpy as jnp
from jax import lax
from jax.sharding import PartitionSpec as P

F32, BF16 = jnp.float32, jnp.bfloat16


def mm(spec, a, b):
    return jnp.einsum(spec, a, b, preferred_element_type=F32)


def layer_apply(u, f, g, k, scales, biases):
    k = k.astype(F32).transpose(0, 2, 1)
    y = mm("cpq,kq->cpk", u, f[0]).astype(BF16)
    h = (mm("jp,cpk->cjk", g[0], y) * k[0]).astype(BF16)
    y = mm("kq,cqp->ckp", f[1], h).astype(BF16)
    wide = u.astype(F32)
    gate = jax.nn.sigmoid(scales[:, None, None] * wide + biases[:, None, None])
    z = (mm("ckp,jp->ckj", y, g[1]) * gate).astype(BF16)
    y = mm("cpq,kq->cpk", z, f[2]).astype(BF16)
    h = (mm("jp,cpk->cjk", g[2], y) * k[1]).astype(BF16)
    y = mm("kq,cqp->ckp", f[3], h).astype(BF16)
    return (wide + mm("ckp,jp->ckj", y, g[3])).astype(BF16)


def local(sequence, first, second, kernels, scale, bias):
    n = lax.axis_size("seq")
    channels = sequence.shape[1] // n
    gather = lambda a: lax.all_gather(a, "segment", axis=0, tiled=True)
    first, second, scale, bias = gather(first), gather(second), gather(scale), gather(bias)
    kernels = lax.all_gather(gather(kernels), "seq", axis=2, tiled=True)
    u = lax.all_to_all(sequence, "seq", split_axis=1, concat_axis=0, tiled=True)
    u = u.transpose(1, 0, 2)
    offset = (lax.axis_index("segment") * n + lax.axis_index("seq")) * channels
    scale = lax.dynamic_slice_in_dim(scale, offset, channels, 1)
    bias = lax.dynamic_slice_in_dim(bias, offset, channels, 1)
    for l in range(first.shape[0]):
        u = layer_apply(u, first[l], second[l], kernels[l], scale[l], bias[l])
    return lax.all_to_all(u.transpose(1, 0, 2), "seq", split_axis=0, concat_axis=1, tiled=True)


def solution(mesh):
    placed = (
        P("seq", "segment", None),
        P("segment", None, None, None),
        P("segment", None, None, None),
        P("segment", None, "seq", None),
        P("segment", None),
        P("segment", None),
    )
    return jax.shard_map(
        local, mesh=mesh, in_specs=placed, out_specs=P("seq", "segment", None), check_vma=False
    )
```

```python
import functools

import jax
import jax.numpy as jnp
from jax import lax
from jax.experimental import pallas as pl
from jax.experimental.pallas import tpu as pltpu
from jax.sharding import PartitionSpec as P

F32, BF16 = jnp.float32, jnp.bfloat16
NT = (((1,), (1,)), ((), ()))
NN = (((1,), (0,)), ((), ()))


def dot(a, b, dims):
    return lax.dot_general(a, b, dims, preferred_element_type=F32)


def kernel(
    n, nz, group, x_in, f_own, g_own, k_own, gate_own, out,
    x, w, kk, gates, kt, gv,
    own_sem, in_send, in_recv, out_send, out_recv, out_own,
    up_send, down_send, z_recv, sib_send, sib_recv, k_send, k_recv,
):
    s, z = lax.axis_index("seq"), lax.axis_index("segment")
    core = lax.rem(s, 2)
    sib = s + 1 - 2 * core
    channels, _, rows, radix = x.shape
    groups = channels // group
    maps = w.shape[2]
    pieces = maps + 2

    def peer(d):
        return lax.rem(s + d, n)

    def remote(src, dst, send, recv, **where):
        return pltpu.make_async_remote_copy(
            src_ref=src, dst_ref=dst, send_sem=send, recv_sem=recv,
            device_id=where, device_id_type=pl.DeviceIdType.MESH,
        )

    def in_copy(g, d):
        t = peer(d)
        here = pl.ds(g * group, group)
        return remote(
            x_in.at[t, here], x.at[here, s], in_send.at[g, d], in_recv.at[g, d], seq=t
        )

    def out_copy(g, d):
        t = peer(d)
        here = pl.ds(g * group, group)
        return remote(
            x.at[here, t], out.at[s, here], out_send.at[g, d], out_recv.at[g, d], seq=t
        )

    def z_views(l):
        return [w.at[core, l, r] for r in range(maps)] + [kk.at[l, s], gates.at[l]]

    def z_copies(l, up):
        sem = up_send if up else down_send
        target = z + 1 if up else z - 1
        return [
            remote(v, v, sem.at[l, i], z_recv.at[l, i], segment=target)
            for i, v in enumerate(z_views(l))
        ]

    def sib_copy(l, r):
        v = w.at[core, l, r]
        return remote(v, v, sib_send.at[l, r], sib_recv.at[l, r], seq=sib)

    def sib_wait(l, r):
        v = w.at[1 - core, l, r]
        remote(v, v, sib_send.at[l, r], sib_recv.at[l, r], seq=sib).wait_recv()

    def k_copy(l, d):
        v = kk.at[l, s]
        return remote(v, v, k_send.at[l, d], k_recv.at[l, d], seq=peer(d))

    def k_wait(l, d):
        v = kk.at[l, lax.rem(s + n - d, n)]
        remote(v, v, k_send.at[l, d], k_recv.at[l, d], seq=peer(d)).wait_recv()

    def in_wait(g, d):
        here = pl.ds(g * group, group)
        v = x.at[here, lax.rem(s + n - d, n)]
        remote(v, v, in_send.at[g, d], in_recv.at[g, d], seq=peer(d)).wait_recv()

    def out_wait(g, d):
        here = pl.ds(g * group, group)
        v = out.at[lax.rem(s + n - d, n), here]
        remote(v, v, out_send.at[g, d], out_recv.at[g, d], seq=peer(d)).wait_recv()

    def k_spread(l):
        def one(d, _):
            k_copy(l, d).start()
            return 0

        lax.fori_loop(1, n, one, 0)

    own = [
        pltpu.make_async_copy(f_own.at[0], w.at[0, z], own_sem.at[0]),
        pltpu.make_async_copy(g_own.at[0], w.at[1, z], own_sem.at[1]),
        pltpu.make_async_copy(k_own.at[0], kk.at[z, s], own_sem.at[2]),
        pltpu.make_async_copy(gate_own.at[0], gates.at[z], own_sem.at[3]),
        pltpu.make_async_copy(x_in.at[s], x.at[:, s], own_sem.at[4]),
    ]
    for c in own:
        c.start()

    barrier = pltpu.get_barrier_semaphore()
    mesh_id = pl.DeviceIdType.MESH

    def greet(d, _):
        pl.semaphore_signal(barrier, inc=1, device_id={"seq": peer(d)}, device_id_type=mesh_id)
        return 0

    lax.fori_loop(1, n, greet, 0)

    @pl.when(z > 0)
    def _():
        pl.semaphore_signal(barrier, inc=1, device_id={"segment": z - 1}, device_id_type=mesh_id)

    @pl.when(z < nz - 1)
    def _():
        pl.semaphore_signal(barrier, inc=1, device_id={"segment": z + 1}, device_id_type=mesh_id)

    beside = (z + nz - 1) // nz + (2 * nz - 2 - z) // nz
    pl.semaphore_wait(barrier, n - 1 + beside)

    for c in own[:4]:
        c.wait()

    @pl.when(z == 0)
    def _():
        for c in z_copies(z, True):
            c.start()

    @pl.when(z > 0)
    def _():
        for c in z_copies(z, False):
            c.start()

    def send_in(g, _):
        def one(d, _):
            in_copy(g, d).start()
            return 0

        lax.fori_loop(1, n, one, 0)

        @pl.when(g == 0)
        def _():
            k_spread(z)

        return 0

    lax.fori_loop(0, groups, send_in, 0)
    own[4].wait()

    def relay(l, up):
        arriving = z_copies(l, up)
        for i, c in enumerate(arriving):
            c.wait_recv()

            @pl.when((z < nz - 1) if up else (z > 0))
            def _():
                c.start()

            if i < maps:
                sib_copy(l, i).start()
            elif i == maps:
                k_spread(l)

    def stage(l):
        @pl.when(z > l)
        def _():
            relay(l, True)

        @pl.when(jnp.logical_and(z == l + 1, z < nz - 1))
        def _():
            for c in z_copies(z, True):
                c.start()

        @pl.when(z + l + 1 < nz)
        def _():
            relay(z + l + 1, False)

        @pl.when(z != l)
        def _():
            for r in range(maps):
                sib_wait(l, r)

        def one(d, _):
            k_wait(l, d)
            return 0

        lax.fori_loop(1, n, one, 0)

    def load(c):
        v = x[c]
        if rows % 16:
            v = v.astype(F32)
        return v.reshape(radix, radix).astype(BF16)

    def store(c, v):
        x[c] = v.reshape(n, rows, radix).astype(BF16)

    total = gates.shape[2]
    first_channel = (z * n + s) * channels

    def prepare(l):
        for i in range(2):
            full = kk[l, :, i].astype(F32).reshape(radix, radix)
            kt[i] = full.T
        pick = lax.broadcasted_iota(jnp.int32, (channels, total), 1) == (
            lax.broadcasted_iota(jnp.int32, (channels, total), 0) + first_channel
        )
        both = gates[l]
        for i in range(2):
            col = jnp.sum(jnp.where(pick, both[i : i + 1], 0.0), axis=1, keepdims=True)
            gv[i] = jnp.broadcast_to(0.5 * col, (channels, radix)).reshape(channels, 1, radix)

    def compute(l, g):
        ids = [g * group + i for i in range(group)]
        f = [w[0, l, r] for r in range(maps)]
        h = [w[1, l, r] for r in range(maps)]
        u = [load(c) for c in ids]
        y = [dot(v, f[0], NT).astype(BF16) for v in u]
        y = [(dot(h[0], v, NN) * kt[0]).astype(BF16) for v in y]
        y = [dot(f[1], v, NN).astype(BF16) for v in y]
        gate = [0.5 + 0.5 * jnp.tanh(gv[0, c] * v.astype(F32) + gv[1, c]) for c, v in zip(ids, u)]
        y = [(dot(v, h[1], NT) * q).astype(BF16) for v, q in zip(y, gate)]
        y = [dot(v, f[2], NT).astype(BF16) for v in y]
        y = [(dot(h[2], v, NN) * kt[1]).astype(BF16) for v in y]
        y = [dot(f[3], v, NN).astype(BF16) for v in y]
        for c, v, base in zip(ids, y, u):
            store(c, base.astype(F32) + dot(v, h[3], NT))

    layers = w.shape[1]

    def layer(l, _):
        stage(l)
        prepare(l)

        def one(g, _):
            @pl.when(l == 0)
            def _():
                def arrive(d, _):
                    in_wait(g, d)
                    return 0

                lax.fori_loop(1, n, arrive, 0)

            compute(l, g)

            @pl.when(l == layers - 1)
            def _():
                def leave(d, _):
                    out_copy(g, d).start()
                    return 0

                lax.fori_loop(1, n, leave, 0)
                here = pl.ds(g * group, group)
                pltpu.make_async_copy(x.at[here, s], out.at[s, here], out_own.at[g]).start()

            return 0

        return lax.fori_loop(0, groups, one, 0)

    lax.fori_loop(0, layers, layer, 0)

    def drain_group(g, _):
        def one(d, _):
            in_copy(g, d).wait_send()
            out_copy(g, d).wait_send()
            out_wait(g, d)
            return 0

        lax.fori_loop(1, n, one, 0)
        here = pl.ds(g * group, group)
        pltpu.make_async_copy(x.at[here, s], out.at[s, here], out_own.at[g]).wait()
        return 0

    lax.fori_loop(0, groups, drain_group, 0)

    def drain_layer(l, _):
        def one(d, _):
            k_copy(l, d).wait_send()
            return 0

        lax.fori_loop(1, n, one, 0)

        @pl.when(z != l)
        def _():
            for r in range(maps):
                sib_copy(l, r).wait_send()

        @pl.when(jnp.logical_and(l <= z, z < nz - 1))
        def _():
            for c in z_copies(l, True):
                c.wait_send()

        @pl.when(jnp.logical_and(l >= z, z > 0))
        def _():
            for c in z_copies(l, False):
                c.wait_send()

        return 0

    lax.fori_loop(0, layers, drain_layer, 0)


def solution(mesh):
    n, nz = mesh.shape["seq"], mesh.shape["segment"]

    def local(sequence, first, second, kernels, scale, bias):
        rows, local_channels, radix = sequence.shape
        channels = local_channels // n
        group = min(4, channels)
        groups = channels // group
        maps = first.shape[1]
        layers = nz
        total = scale.shape[1]
        x_in = sequence.transpose(1, 0, 2).reshape(n, channels, rows, radix)
        gate = jnp.stack([scale, bias], axis=1)
        sem = pltpu.SemaphoreType.DMA
        anywhere = pl.BlockSpec(memory_space=pl.ANY)
        result = pl.pallas_call(
            functools.partial(kernel, n, nz, group),
            out_shape=jax.ShapeDtypeStruct((n, channels, rows, radix), BF16),
            in_specs=[anywhere] * 5,
            out_specs=anywhere,
            scratch_shapes=[
                pltpu.VMEM((channels, n, rows, radix), BF16),
                pltpu.VMEM((2, layers, maps, radix, radix), BF16),
                pltpu.VMEM((layers, n, 2, rows, radix), BF16),
                pltpu.VMEM((layers, 2, total), F32),
                pltpu.VMEM((2, radix, radix), F32),
                pltpu.VMEM((2, channels, 1, radix), F32),
                sem((5,)),
                sem((groups, n)),
                sem((groups, n)),
                sem((groups, n)),
                sem((groups, n)),
                sem((groups,)),
                sem((layers, maps + 2)),
                sem((layers, maps + 2)),
                sem((layers, maps + 2)),
                sem((layers, maps)),
                sem((layers, maps)),
                sem((layers, n)),
                sem((layers, n)),
            ],
            compiler_params=pltpu.CompilerParams(
                collective_id=0, has_side_effects=True, vmem_limit_bytes=56 * 2**20
            ),
        )(x_in, first, second, kernels, gate)
        return result.reshape(local_channels, rows, radix).transpose(1, 0, 2)

    placed = (
        P("seq", "segment", None),
        P("segment", None, None, None),
        P("segment", None, None, None),
        P("segment", None, "seq", None),
        P("segment", None),
        P("segment", None),
    )
    return jax.shard_map(
        local, mesh=mesh, in_specs=placed, out_specs=P("seq", "segment", None), check_vma=False
    )
```

```python
import functools

import jax
import jax.numpy as jnp
from jax import lax
from jax.experimental import pallas as pl
from jax.experimental.pallas import tpu as pltpu
from jax.sharding import PartitionSpec as P

F32, BF16 = jnp.float32, jnp.bfloat16
NT = (((1,), (1,)), ((), ()))
NN = (((1,), (0,)), ((), ()))


def dot(a, b, dims):
    return lax.dot_general(a, b, dims, preferred_element_type=F32)


def kernel(
    n, nz, group, x_in, f_own, g_own, k_own, gate_own, out,
    x, w, kk, gates, kt, gv,
    own_sem, in_send, in_recv, out_send, out_recv, out_own,
    up_send, down_send, z_recv, sib_send, sib_recv,
    kz_send, kz_recv, gz_send, gz_recv, ks_send, ks_recv, kf_send, kf_recv,
):
    s, z = lax.axis_index("seq"), lax.axis_index("segment")
    core = lax.rem(s, 2)
    sib = s + 1 - 2 * core
    channels, _, rows, radix = x.shape
    groups = channels // group
    maps = w.shape[2]
    layers = w.shape[1]
    half = n // 2

    def peer(d):
        return lax.rem(s + d, n)

    def remote(src, dst, send, recv, **where):
        return pltpu.make_async_remote_copy(
            src_ref=src, dst_ref=dst, send_sem=send, recv_sem=recv,
            device_id=where, device_id_type=pl.DeviceIdType.MESH,
        )

    def in_copy(g, d):
        t = peer(d)
        here = pl.ds(g * group, group)
        return remote(
            x_in.at[t, here], x.at[here, s], in_send.at[g, d], in_recv.at[g, d], seq=t
        )

    def out_copy(g, d):
        t = peer(d)
        here = pl.ds(g * group, group)
        return remote(
            x.at[here, t], out.at[s, here], out_send.at[g, d], out_recv.at[g, d], seq=t
        )

    def z_copy(l, i, up):
        v = w.at[core, l, i]
        sem = up_send if up else down_send
        return remote(v, v, sem.at[l, i], z_recv.at[l, i], segment=z + 1 if up else z - 1)

    def sib_copy(l, r):
        v = w.at[core, l, r]
        return remote(v, v, sib_send.at[l, r], sib_recv.at[l, r], seq=sib)

    def sib_wait(l, r):
        v = w.at[1 - core, l, r]
        remote(v, v, sib_send.at[l, r], sib_recv.at[l, r], seq=sib).wait_recv()

    def kz_copy(d, l):
        to = lax.rem(z + d, nz)
        return (
            remote(kk.at[s, l], kk.at[s, l], kz_send.at[d], kz_recv.at[d], segment=to),
            remote(gates.at[l], gates.at[l], gz_send.at[d], gz_recv.at[d], segment=to),
        )

    def ks_copy(d, owner):
        v = kk.at[owner]
        return remote(v, v, ks_send.at[d], ks_recv.at[d], seq=lax.rem(s + 2 * d, n))

    def kf_copy(d, owner):
        v = kk.at[owner]
        return remote(v, v, kf_send.at[d], kf_recv.at[d], seq=sib)

    def in_wait(g, d):
        here = pl.ds(g * group, group)
        v = x.at[here, lax.rem(s + n - d, n)]
        remote(v, v, in_send.at[g, d], in_recv.at[g, d], seq=peer(d)).wait_recv()

    def out_wait(g, d):
        here = pl.ds(g * group, group)
        v = out.at[lax.rem(s + n - d, n), here]
        remote(v, v, out_send.at[g, d], out_recv.at[g, d], seq=peer(d)).wait_recv()

    own = [
        pltpu.make_async_copy(f_own.at[0], w.at[0, z], own_sem.at[0]),
        pltpu.make_async_copy(g_own.at[0], w.at[1, z], own_sem.at[1]),
        pltpu.make_async_copy(k_own.at[0], kk.at[s, z], own_sem.at[2]),
        pltpu.make_async_copy(gate_own.at[0], gates.at[z], own_sem.at[3]),
        pltpu.make_async_copy(x_in.at[s], x.at[:, s], own_sem.at[4]),
    ]
    for c in own:
        c.start()

    barrier = pltpu.get_barrier_semaphore()
    mesh_id = pl.DeviceIdType.MESH

    def greet(d, _):
        pl.semaphore_signal(barrier, inc=1, device_id={"seq": peer(d)}, device_id_type=mesh_id)
        return 0

    lax.fori_loop(1, n, greet, 0)

    def greet_z(d, _):
        to = lax.rem(z + d, nz)
        pl.semaphore_signal(barrier, inc=1, device_id={"segment": to}, device_id_type=mesh_id)
        return 0

    lax.fori_loop(1, nz, greet_z, 0)
    pl.semaphore_wait(barrier, n + nz - 2)

    for c in own[:4]:
        c.wait()

    for d in range(1, nz):
        for c in kz_copy(d, z):
            c.start()

    def send_in(g, _):
        def one(d, _):
            in_copy(g, d).start()
            return 0

        return lax.fori_loop(1, n, one, 0)

    send_in(0, 0)

    def send_own(up):
        for i in range(maps):
            z_copy(z, i, up).start()

    @pl.when(z == 0)
    def _():
        send_own(True)

    @pl.when(z > 0)
    def _():
        send_own(False)

    for d in range(1, nz):
        for c in kz_copy(d, lax.rem(z + nz - d, nz)):
            c.wait_recv()
    for d in range(1, half):
        ks_copy(d, s).start()
    kf_copy(0, s).start()
    lax.fori_loop(1, groups, send_in, 0)
    own[4].wait()

    def relay(l, i, up):
        c = z_copy(l, i, up)
        c.wait_recv()

        @pl.when((z < nz - 1) if up else (z > 0))
        def _():
            c.start()

        sib_copy(l, i).start()

    def stage(k, i):
        @pl.when(z > k)
        def _():
            relay(k, i, True)

        @pl.when(z + k + 1 < nz)
        def _():
            relay(z + k + 1, i, False)

    def stage_end(k):
        @pl.when(jnp.logical_and(z == k + 1, z < nz - 1))
        def _():
            send_own(True)

    def sib_arrive(l):
        @pl.when(z != l)
        def _():
            for r in range(maps):
                sib_wait(l, r)

    for i in range(maps):
        stage(0, i)
    stage_end(0)

    def load(c):
        v = x[c]
        if rows % 16:
            v = v.astype(F32)
        return v.reshape(radix, radix).astype(BF16)

    def store(c, v):
        x[c] = v.reshape(n, rows, radix).astype(BF16)

    total = gates.shape[2]
    first_channel = (z * n + s) * channels

    def prepare(l, _):
        for i in range(2):
            full = kk[:, l, i].astype(F32).reshape(radix, radix)
            kt[l, i] = full.T
        pick = lax.broadcasted_iota(jnp.int32, (channels, total), 1) == (
            lax.broadcasted_iota(jnp.int32, (channels, total), 0) + first_channel
        )
        both = gates[l]
        for i in range(2):
            col = jnp.sum(jnp.where(pick, both[i : i + 1], 0.0), axis=1, keepdims=True)
            wide = jnp.broadcast_to(0.5 * col, (channels, radix))
            gv[l, i] = wide.reshape(channels, 1, radix)
        return 0

    def compute(l, g):
        ids = [g * group + i for i in range(group)]
        f = [w[0, l, r] for r in range(maps)]
        h = [w[1, l, r] for r in range(maps)]
        u = [load(c) for c in ids]
        y = [dot(v, f[0], NT).astype(BF16) for v in u]
        y = [(dot(h[0], v, NN) * kt[l, 0]).astype(BF16) for v in y]
        y = [dot(f[1], v, NN).astype(BF16) for v in y]
        gate = [0.5 + 0.5 * jnp.tanh(gv[l, 0, c] * v.astype(F32) + gv[l, 1, c]) for c, v in zip(ids, u)]
        y = [(dot(v, h[1], NT) * q).astype(BF16) for v, q in zip(y, gate)]
        y = [dot(v, f[2], NT).astype(BF16) for v in y]
        y = [(dot(h[2], v, NN) * kt[l, 1]).astype(BF16) for v in y]
        y = [dot(f[3], v, NN).astype(BF16) for v in y]
        for c, v, base in zip(ids, y, u):
            store(c, base.astype(F32) + dot(v, h[3], NT))

    for d in range(1, half):
        ks_copy(d, lax.rem(s + n - 2 * d, n)).wait_recv()
        kf_copy(d, lax.rem(s + n - 2 * d, n)).start()
    for d in range(half):
        kf_copy(d, lax.rem(sib + n - 2 * d, n)).wait_recv()
    lax.fori_loop(0, layers, prepare, 0)

    def step(l, g):
        @pl.when(l == 0)
        def _():
            def arrive(d, _):
                in_wait(g, d)
                return 0

            lax.fori_loop(1, n, arrive, 0)

        compute(l, g)

        @pl.when(l == layers - 1)
        def _():
            def leave(d, _):
                out_copy(g, d).start()
                return 0

            lax.fori_loop(1, n, leave, 0)
            here = pl.ds(g * group, group)
            pltpu.make_async_copy(x.at[here, s], out.at[s, here], out_own.at[g]).start()

    per = maps // groups if maps % groups == 0 else maps
    whole = layers - 2 if layers > 2 else layers

    def layer(l, _):
        sib_arrive(l)

        def one(g, _):
            step(l, g)

            @pl.when(jnp.logical_and(l + 1 < nz - 1, g * per < maps))
            def _():
                for j in range(per):
                    stage(l + 1, g * per + j)

            return 0

        lax.fori_loop(0, groups, one, 0)

        @pl.when(l + 1 < nz - 1)
        def _():
            stage_end(l + 1)

        return 0

    lax.fori_loop(0, whole, layer, 0)

    def last(g, _):
        def one(l, _):
            @pl.when(g == 0)
            def _():
                sib_arrive(l)

            step(l, g)
            return 0

        return lax.fori_loop(whole, layers, one, 0)

    lax.fori_loop(0, groups, last, 0)

    def drain_group(g, _):
        def one(d, _):
            in_copy(g, d).wait_send()
            out_copy(g, d).wait_send()
            out_wait(g, d)
            return 0

        lax.fori_loop(1, n, one, 0)
        here = pl.ds(g * group, group)
        pltpu.make_async_copy(x.at[here, s], out.at[s, here], out_own.at[g]).wait()
        return 0

    lax.fori_loop(0, groups, drain_group, 0)

    for d in range(1, nz):
        for c in kz_copy(d, z):
            c.wait_send()
    for d in range(1, half):
        ks_copy(d, s).wait_send()
    for d in range(half):
        kf_copy(d, lax.rem(s + n - 2 * d, n)).wait_send()

    def drain_layer(l, _):
        @pl.when(z != l)
        def _():
            for r in range(maps):
                sib_copy(l, r).wait_send()

        @pl.when(jnp.logical_and(l <= z, z < nz - 1))
        def _():
            for r in range(maps):
                z_copy(l, r, True).wait_send()

        @pl.when(jnp.logical_and(l >= z, z > 0))
        def _():
            for r in range(maps):
                z_copy(l, r, False).wait_send()

        return 0

    lax.fori_loop(0, layers, drain_layer, 0)


def solution(mesh):
    n, nz = mesh.shape["seq"], mesh.shape["segment"]

    def local(sequence, first, second, kernels, scale, bias):
        rows, local_channels, radix = sequence.shape
        channels = local_channels // n
        group = min(4, channels)
        groups = channels // group
        maps = first.shape[1]
        layers = nz
        total = scale.shape[1]
        x_in = sequence.transpose(1, 0, 2).reshape(n, channels, rows, radix)
        gate = jnp.stack([scale, bias], axis=1)
        sem = pltpu.SemaphoreType.DMA
        anywhere = pl.BlockSpec(memory_space=pl.ANY)
        result = pl.pallas_call(
            functools.partial(kernel, n, nz, group),
            out_shape=jax.ShapeDtypeStruct((n, channels, rows, radix), BF16),
            in_specs=[anywhere] * 5,
            out_specs=anywhere,
            scratch_shapes=[
                pltpu.VMEM((channels, n, rows, radix), BF16),
                pltpu.VMEM((2, layers, maps, radix, radix), BF16),
                pltpu.VMEM((n, layers, 2, rows, radix), BF16),
                pltpu.VMEM((layers, 2, total), F32),
                pltpu.VMEM((layers, 2, radix, radix), F32),
                pltpu.VMEM((layers, 2, channels, 1, radix), F32),
                sem((5,)),
                sem((groups, n)),
                sem((groups, n)),
                sem((groups, n)),
                sem((groups, n)),
                sem((groups,)),
                sem((layers, maps)),
                sem((layers, maps)),
                sem((layers, maps)),
                sem((layers, maps)),
                sem((layers, maps)),
                sem((nz,)),
                sem((nz,)),
                sem((nz,)),
                sem((nz,)),
                sem((n // 2,)),
                sem((n // 2,)),
                sem((n // 2,)),
                sem((n // 2,)),
            ],
            compiler_params=pltpu.CompilerParams(
                collective_id=0, has_side_effects=True, vmem_limit_bytes=56 * 2**20
            ),
        )(x_in, first, second, kernels, gate)
        return result.reshape(local_channels, rows, radix).transpose(1, 0, 2)

    placed = (
        P("seq", "segment", None),
        P("segment", None, None, None),
        P("segment", None, None, None),
        P("segment", None, "seq", None),
        P("segment", None),
        P("segment", None),
    )
    return jax.shard_map(
        local, mesh=mesh, in_specs=placed, out_specs=P("seq", "segment", None), check_vma=False
    )
```

```python
import functools

import jax
import jax.numpy as jnp
from jax import lax
from jax.experimental import pallas as pl
from jax.experimental.pallas import tpu as pltpu
from jax.sharding import PartitionSpec as P

F32, BF16 = jnp.float32, jnp.bfloat16
NT = (((1,), (1,)), ((), ()))
NN = (((1,), (0,)), ((), ()))


def dot(a, b, dims):
    return lax.dot_general(a, b, dims, preferred_element_type=F32)


def kernel(
    n, nz, group, x_in, f_own, g_own, k_own, scale_own, bias_own, out,
    x, w, kk, scales, biases, kt, gv,
    own_sem, in_send, in_recv, out_send, out_recv, out_own,
    up_send, down_send, z_recv, sib_send, sib_recv,
    kz_send, kz_recv, gz_send, gz_recv, bz_send, bz_recv, ks_send, ks_recv, kf_send, kf_recv,
):
    s, z = lax.axis_index("seq"), lax.axis_index("segment")
    core = lax.rem(s, 2)
    sib = s + 1 - 2 * core
    channels, _, rows, radix = x.shape
    groups = channels // group
    maps = w.shape[2]
    layers = w.shape[1]
    half = n // 2

    def peer(d):
        return lax.rem(s + d, n)

    def remote(src, dst, send, recv, **where):
        return pltpu.make_async_remote_copy(
            src_ref=src, dst_ref=dst, send_sem=send, recv_sem=recv,
            device_id=where, device_id_type=pl.DeviceIdType.MESH,
        )

    def in_copy(g, d):
        t = peer(d)
        here = pl.ds(g * group, group)
        return remote(
            x_in.at[t, here], x.at[here, s], in_send.at[g, d], in_recv.at[g, d], seq=t
        )

    def out_copy(g, d):
        t = peer(d)
        here = pl.ds(g * group, group)
        return remote(
            x.at[here, t], out.at[s, here], out_send.at[g, d], out_recv.at[g, d], seq=t
        )

    def z_copy(l, i, up):
        v = w.at[core, l, i]
        sem = up_send if up else down_send
        return remote(v, v, sem.at[l, i], z_recv.at[l, i], segment=z + 1 if up else z - 1)

    def sib_copy(l, r):
        v = w.at[core, l, r]
        return remote(v, v, sib_send.at[l, r], sib_recv.at[l, r], seq=sib)

    def sib_wait(l, r):
        v = w.at[1 - core, l, r]
        remote(v, v, sib_send.at[l, r], sib_recv.at[l, r], seq=sib).wait_recv()

    def kz_copy(d, l):
        to = lax.rem(z + d, nz)
        return (
            remote(kk.at[s, l], kk.at[s, l], kz_send.at[d], kz_recv.at[d], segment=to),
            remote(scales.at[l], scales.at[l], gz_send.at[d], gz_recv.at[d], segment=to),
            remote(biases.at[l], biases.at[l], bz_send.at[d], bz_recv.at[d], segment=to),
        )

    def ks_copy(d, owner):
        v = kk.at[owner]
        return remote(v, v, ks_send.at[d], ks_recv.at[d], seq=lax.rem(s + 2 * d, n))

    def kf_copy(d, owner):
        v = kk.at[owner]
        return remote(v, v, kf_send.at[d], kf_recv.at[d], seq=sib)

    def in_wait(g, d):
        here = pl.ds(g * group, group)
        v = x.at[here, lax.rem(s + n - d, n)]
        remote(v, v, in_send.at[g, d], in_recv.at[g, d], seq=peer(d)).wait_recv()

    def out_wait(g, d):
        here = pl.ds(g * group, group)
        v = out.at[lax.rem(s + n - d, n), here]
        remote(v, v, out_send.at[g, d], out_recv.at[g, d], seq=peer(d)).wait_recv()

    own = [
        pltpu.make_async_copy(f_own.at[0], w.at[0, z], own_sem.at[0]),
        pltpu.make_async_copy(g_own.at[0], w.at[1, z], own_sem.at[1]),
        pltpu.make_async_copy(k_own.at[0], kk.at[s, z], own_sem.at[2]),
        pltpu.make_async_copy(scale_own, scales.at[z], own_sem.at[3]),
        pltpu.make_async_copy(bias_own, biases.at[z], own_sem.at[4]),
        pltpu.make_async_copy(x_in.at[s], x.at[:, s], own_sem.at[5]),
    ]
    for c in own:
        c.start()

    barrier = pltpu.get_barrier_semaphore()
    mesh_id = pl.DeviceIdType.MESH

    def greet(d, _):
        pl.semaphore_signal(barrier, inc=1, device_id={"seq": peer(d)}, device_id_type=mesh_id)
        return 0

    lax.fori_loop(1, n, greet, 0)

    def greet_z(d, _):
        to = lax.rem(z + d, nz)
        pl.semaphore_signal(barrier, inc=1, device_id={"segment": to}, device_id_type=mesh_id)
        return 0

    lax.fori_loop(1, nz, greet_z, 0)
    pl.semaphore_wait(barrier, n + nz - 2)

    for c in own[:5]:
        c.wait()

    for d in range(1, nz):
        for c in kz_copy(d, z):
            c.start()

    def send_in(g, _):
        def one(d, _):
            in_copy(g, d).start()
            return 0

        return lax.fori_loop(1, n, one, 0)

    send_in(0, 0)

    def send_own(up):
        for i in range(maps):
            z_copy(z, i, up).start()

    @pl.when(jnp.logical_and(z != 1, z < nz - 1))
    def _():
        send_own(True)

    @pl.when(z > 0)
    def _():
        send_own(False)

    for d in range(1, nz):
        for c in kz_copy(d, lax.rem(z + nz - d, nz)):
            c.wait_recv()
    for d in range(1, half):
        ks_copy(d, s).start()
    kf_copy(0, s).start()
    lax.fori_loop(1, groups, send_in, 0)
    own[5].wait()

    def relay(l, i, up):
        c = z_copy(l, i, up)
        c.wait_recv()

        @pl.when((z < nz - 1) if up else (z > 0))
        def _():
            c.start()

        sib_copy(l, i).start()

    def stage(k, i):
        @pl.when(z > k)
        def _():
            relay(k, i, True)

        @pl.when(z + k + 1 < nz)
        def _():
            relay(z + k + 1, i, False)

    def sib_arrive(l):
        @pl.when(z != l)
        def _():
            for r in range(maps):
                sib_wait(l, r)

    for i in range(maps):
        stage(0, i)

    @pl.when(jnp.logical_and(z == 1, z < nz - 1))
    def _():
        send_own(True)

    def load(c):
        v = x[c]
        if rows % 16:
            v = v.astype(F32)
        return v.reshape(radix, radix).astype(BF16)

    def store(c, v):
        x[c] = v.reshape(n, rows, radix).astype(BF16)

    total = scales.shape[2]
    first_channel = (z * n + s) * channels

    def prepare(l, _):
        for i in range(2):
            full = kk[:, l, i].astype(F32).reshape(radix, radix)
            kt[l, i] = full.T
        pick = lax.broadcasted_iota(jnp.int32, (channels, total), 1) == (
            lax.broadcasted_iota(jnp.int32, (channels, total), 0) + first_channel
        )
        for i, values in enumerate((scales[l], biases[l])):
            col = jnp.sum(jnp.where(pick, values, 0.0), axis=1, keepdims=True)
            wide = jnp.broadcast_to(0.5 * col, (channels, radix))
            gv[l, i] = wide.reshape(channels, 1, radix)
        return 0

    def compute(l, g):
        ids = [g * group + i for i in range(group)]
        f = [w[0, l, r] for r in range(maps)]
        h = [w[1, l, r] for r in range(maps)]
        u = [load(c) for c in ids]
        y = [dot(v, f[0], NT).astype(BF16) for v in u]
        y = [(dot(h[0], v, NN) * kt[l, 0]).astype(BF16) for v in y]
        y = [dot(f[1], v, NN).astype(BF16) for v in y]
        gate = [0.5 + 0.5 * jnp.tanh(gv[l, 0, c] * v.astype(F32) + gv[l, 1, c]) for c, v in zip(ids, u)]
        y = [(dot(v, h[1], NT) * q).astype(BF16) for v, q in zip(y, gate)]
        y = [dot(v, f[2], NT).astype(BF16) for v in y]
        y = [(dot(h[2], v, NN) * kt[l, 1]).astype(BF16) for v in y]
        y = [dot(f[3], v, NN).astype(BF16) for v in y]
        for c, v, base in zip(ids, y, u):
            store(c, base.astype(F32) + dot(v, h[3], NT))

    for d in range(1, half):
        ks_copy(d, lax.rem(s + n - 2 * d, n)).wait_recv()
        kf_copy(d, lax.rem(s + n - 2 * d, n)).start()
    for d in range(half):
        kf_copy(d, lax.rem(sib + n - 2 * d, n)).wait_recv()
    lax.fori_loop(0, layers, prepare, 0)

    def step(l, g):
        @pl.when(l == 0)
        def _():
            def arrive(d, _):
                in_wait(g, d)
                return 0

            lax.fori_loop(1, n, arrive, 0)

        compute(l, g)

        @pl.when(l == layers - 1)
        def _():
            def leave(d, _):
                out_copy(g, d).start()
                return 0

            lax.fori_loop(1, n, leave, 0)
            here = pl.ds(g * group, group)
            pltpu.make_async_copy(x.at[here, s], out.at[s, here], out_own.at[g]).start()

    per = maps // groups if maps % groups == 0 else maps
    whole = max(layers - 3, 1)

    def layer(l, _):
        sib_arrive(l)

        def one(g, _):
            step(l, g)

            @pl.when(jnp.logical_and(l + 1 < nz - 1, g * per < maps))
            def _():
                for j in range(per):
                    stage(l + 1, g * per + j)

            return 0

        lax.fori_loop(0, groups, one, 0)

        return 0

    lax.fori_loop(0, whole, layer, 0)

    def last(g, _):
        def one(l, _):
            @pl.when(jnp.logical_and(g == 0, jnp.logical_and(l > whole, l < nz - 1)))
            def _():
                for i in range(maps):
                    stage(l, i)

            @pl.when(g == 0)
            def _():
                sib_arrive(l)

            step(l, g)
            return 0

        return lax.fori_loop(whole, layers, one, 0)

    lax.fori_loop(0, groups, last, 0)

    def drain_group(g, _):
        def one(d, _):
            in_copy(g, d).wait_send()
            out_copy(g, d).wait_send()
            out_wait(g, d)
            return 0

        lax.fori_loop(1, n, one, 0)
        here = pl.ds(g * group, group)
        pltpu.make_async_copy(x.at[here, s], out.at[s, here], out_own.at[g]).wait()
        return 0

    lax.fori_loop(0, groups, drain_group, 0)

    for d in range(1, nz):
        for c in kz_copy(d, z):
            c.wait_send()
    for d in range(1, half):
        ks_copy(d, s).wait_send()
    for d in range(half):
        kf_copy(d, lax.rem(s + n - 2 * d, n)).wait_send()

    def drain_layer(l, _):
        @pl.when(z != l)
        def _():
            for r in range(maps):
                sib_copy(l, r).wait_send()

        @pl.when(jnp.logical_and(l <= z, z < nz - 1))
        def _():
            for r in range(maps):
                z_copy(l, r, True).wait_send()

        @pl.when(jnp.logical_and(l >= z, z > 0))
        def _():
            for r in range(maps):
                z_copy(l, r, False).wait_send()

        return 0

    lax.fori_loop(0, layers, drain_layer, 0)


def solution(mesh):
    n, nz = mesh.shape["seq"], mesh.shape["segment"]

    def local(sequence, first, second, kernels, scale, bias):
        rows, local_channels, radix = sequence.shape
        channels = local_channels // n
        group = min(4, channels)
        groups = channels // group
        maps = first.shape[1]
        layers = nz
        total = scale.shape[1]
        x_in = sequence.transpose(1, 0, 2).reshape(n, channels, rows, radix)
        sem = pltpu.SemaphoreType.DMA
        anywhere = pl.BlockSpec(memory_space=pl.ANY)
        result = pl.pallas_call(
            functools.partial(kernel, n, nz, group),
            out_shape=jax.ShapeDtypeStruct((n, channels, rows, radix), BF16),
            in_specs=[anywhere] * 6,
            out_specs=anywhere,
            scratch_shapes=[
                pltpu.VMEM((channels, n, rows, radix), BF16),
                pltpu.VMEM((2, layers, maps, radix, radix), BF16),
                pltpu.VMEM((n, layers, 2, rows, radix), BF16),
                pltpu.VMEM((layers, 1, total), F32),
                pltpu.VMEM((layers, 1, total), F32),
                pltpu.VMEM((layers, 2, radix, radix), F32),
                pltpu.VMEM((layers, 2, channels, 1, radix), F32),
                sem((6,)),
                sem((groups, n)),
                sem((groups, n)),
                sem((groups, n)),
                sem((groups, n)),
                sem((groups,)),
                sem((layers, maps)),
                sem((layers, maps)),
                sem((layers, maps)),
                sem((layers, maps)),
                sem((layers, maps)),
                sem((nz,)),
                sem((nz,)),
                sem((nz,)),
                sem((nz,)),
                sem((nz,)),
                sem((nz,)),
                sem((n // 2,)),
                sem((n // 2,)),
                sem((n // 2,)),
                sem((n // 2,)),
            ],
            compiler_params=pltpu.CompilerParams(
                collective_id=0, has_side_effects=True, vmem_limit_bytes=56 * 2**20
            ),
        )(x_in, first, second, kernels, scale, bias)
        return result.reshape(local_channels, rows, radix).transpose(1, 0, 2)

    placed = (
        P("seq", "segment", None),
        P("segment", None, None, None),
        P("segment", None, None, None),
        P("segment", None, "seq", None),
        P("segment", None),
        P("segment", None),
    )
    return jax.shard_map(
        local, mesh=mesh, in_specs=placed, out_specs=P("seq", "segment", None), check_vma=False
    )
```

```python
import functools

import jax
import jax.numpy as jnp
from jax import lax
from jax.experimental import pallas as pl
from jax.experimental.pallas import tpu as pltpu
from jax.sharding import PartitionSpec as P

F32, BF16 = jnp.float32, jnp.bfloat16
NT = (((1,), (1,)), ((), ()))
NN = (((1,), (0,)), ((), ()))


def dot(a, b, dims):
    return lax.dot_general(a, b, dims, preferred_element_type=F32)


def kernel(
    n, nz, group, seq_in, f_own, g_own, k_own, scale_own, bias_own, out,
    raw, x_in, x, w, kk, scales, biases, kt, gv,
    own_sem, raw_sem, in_send, in_recv, out_send, out_recv, out_own,
    up_send, down_send, z_recv, sib_send, sib_recv,
    kz_send, kz_recv, gz_send, gz_recv, bz_send, bz_recv, ks_send, ks_recv, kf_send, kf_recv,
):
    s, z = lax.axis_index("seq"), lax.axis_index("segment")
    core = lax.rem(s, 2)
    sib = s + 1 - 2 * core
    channels, _, rows, radix = x.shape
    groups = channels // group
    maps = w.shape[2]
    layers = w.shape[1]
    half = n // 2

    def peer(d):
        return lax.rem(s + d, n)

    def remote(src, dst, send, recv, **where):
        return pltpu.make_async_remote_copy(
            src_ref=src, dst_ref=dst, send_sem=send, recv_sem=recv,
            device_id=where, device_id_type=pl.DeviceIdType.MESH,
        )

    def in_copy(g, d):
        t = peer(d)
        here = pl.ds(g * group, group)
        return remote(
            x_in.at[t, here], x.at[here, s], in_send.at[g, d], in_recv.at[g, d], seq=t
        )

    def out_copy(g, d):
        t = peer(d)
        here = pl.ds(g * group, group)
        return remote(
            x.at[here, t], out.at[s, here], out_send.at[g, d], out_recv.at[g, d], seq=t
        )

    def z_copy(l, i, up):
        v = w.at[core, l, i]
        sem = up_send if up else down_send
        return remote(v, v, sem.at[l, i], z_recv.at[l, i], segment=z + 1 if up else z - 1)

    def sib_copy(l, r):
        v = w.at[core, l, r]
        return remote(v, v, sib_send.at[l, r], sib_recv.at[l, r], seq=sib)

    def sib_wait(l, r):
        v = w.at[1 - core, l, r]
        remote(v, v, sib_send.at[l, r], sib_recv.at[l, r], seq=sib).wait_recv()

    def kz_copy(d, l):
        to = lax.rem(z + d, nz)
        return (
            remote(kk.at[s, l], kk.at[s, l], kz_send.at[d], kz_recv.at[d], segment=to),
            remote(scales.at[l], scales.at[l], gz_send.at[d], gz_recv.at[d], segment=to),
            remote(biases.at[l], biases.at[l], bz_send.at[d], bz_recv.at[d], segment=to),
        )

    def ks_copy(d, owner):
        v = kk.at[owner]
        return remote(v, v, ks_send.at[d], ks_recv.at[d], seq=lax.rem(s + 2 * d, n))

    def kf_copy(d, owner):
        v = kk.at[owner]
        return remote(v, v, kf_send.at[d], kf_recv.at[d], seq=sib)

    def in_wait(g, d):
        here = pl.ds(g * group, group)
        v = x.at[here, lax.rem(s + n - d, n)]
        remote(v, v, in_send.at[g, d], in_recv.at[g, d], seq=peer(d)).wait_recv()

    def out_wait(g, d):
        here = pl.ds(g * group, group)
        v = out.at[lax.rem(s + n - d, n), here]
        remote(v, v, out_send.at[g, d], out_recv.at[g, d], seq=peer(d)).wait_recv()

    own = [
        pltpu.make_async_copy(f_own.at[0], w.at[0, z], own_sem.at[0]),
        pltpu.make_async_copy(g_own.at[0], w.at[1, z], own_sem.at[1]),
        pltpu.make_async_copy(k_own.at[0], kk.at[s, z], own_sem.at[2]),
        pltpu.make_async_copy(scale_own, scales.at[z], own_sem.at[3]),
        pltpu.make_async_copy(bias_own, biases.at[z], own_sem.at[4]),
    ]
    def raw_copy(d):
        t = peer(d)
        return pltpu.make_async_copy(seq_in.at[:, t], raw.at[t], raw_sem.at[d])

    for c in own:
        c.start()
    for d in range(1, n + 1):
        raw_copy(d % n).start()

    barrier = pltpu.get_barrier_semaphore()
    mesh_id = pl.DeviceIdType.MESH

    def greet(d, _):
        pl.semaphore_signal(barrier, inc=1, device_id={"seq": peer(d)}, device_id_type=mesh_id)
        return 0

    lax.fori_loop(1, n, greet, 0)

    def greet_z(d, _):
        to = lax.rem(z + d, nz)
        pl.semaphore_signal(barrier, inc=1, device_id={"segment": to}, device_id_type=mesh_id)
        return 0

    lax.fori_loop(1, nz, greet_z, 0)
    pl.semaphore_wait(barrier, n + nz - 2)

    for c in own:
        c.wait()

    for d in range(1, nz):
        for c in kz_copy(d, z):
            c.start()

    def send_in(g, _):
        def one(d, _):
            in_copy(g, d).start()
            return 0

        return lax.fori_loop(1, n, one, 0)

    def turned(d):
        raw_copy(d).wait()
        v = raw[peer(d)]
        return jnp.swapaxes(v, 0, 1)

    def turn(d, _):
        x_in[peer(d)] = turned(d)

        @pl.when(d > 1)
        def _():
            in_copy(0, d - 1).start()

        return 0

    def send_own(up):
        for i in range(maps):
            z_copy(z, i, up).start()

    @pl.when(jnp.logical_and(z != 1, z < nz - 1))
    def _():
        send_own(True)

    @pl.when(z > 0)
    def _():
        send_own(False)

    lax.fori_loop(1, n, turn, 0)
    x[:, pl.ds(s, 1)] = turned(0)[:, None]
    in_copy(0, n - 1).start()

    for d in range(1, nz):
        for c in kz_copy(d, lax.rem(z + nz - d, nz)):
            c.wait_recv()
    for d in range(1, half):
        ks_copy(d, s).start()
    kf_copy(0, s).start()
    lax.fori_loop(1, groups, send_in, 0)

    def relay(l, i, up):
        c = z_copy(l, i, up)
        c.wait_recv()

        @pl.when((z < nz - 1) if up else (z > 0))
        def _():
            c.start()

        sib_copy(l, i).start()

    def stage(k, i):
        @pl.when(z > k)
        def _():
            relay(k, i, True)

        @pl.when(z + k + 1 < nz)
        def _():
            relay(z + k + 1, i, False)

    def sib_arrive(l):
        @pl.when(z != l)
        def _():
            for r in range(maps):
                sib_wait(l, r)

    for i in range(maps):
        stage(0, i)

    @pl.when(jnp.logical_and(z == 1, z < nz - 1))
    def _():
        send_own(True)

    def load(c):
        v = x[c]
        if rows % 16:
            v = v.astype(F32)
        return v.reshape(radix, radix).astype(BF16)

    def store(c, v):
        x[c] = v.reshape(n, rows, radix).astype(BF16)

    total = scales.shape[2]
    first_channel = (z * n + s) * channels

    def prepare(l, _):
        for i in range(2):
            full = kk[:, l, i].astype(F32).reshape(radix, radix)
            kt[l, i] = full.T
        pick = lax.broadcasted_iota(jnp.int32, (channels, total), 1) == (
            lax.broadcasted_iota(jnp.int32, (channels, total), 0) + first_channel
        )
        for i, values in enumerate((scales[l], biases[l])):
            col = jnp.sum(jnp.where(pick, values, 0.0), axis=1, keepdims=True)
            wide = jnp.broadcast_to(0.5 * col, (channels, radix))
            gv[l, i] = wide.reshape(channels, 1, radix)
        return 0

    def compute(l, g):
        ids = [g * group + i for i in range(group)]
        f = [w[0, l, r] for r in range(maps)]
        h = [w[1, l, r] for r in range(maps)]
        u = [load(c) for c in ids]
        y = [dot(v, f[0], NT).astype(BF16) for v in u]
        y = [(dot(h[0], v, NN) * kt[l, 0]).astype(BF16) for v in y]
        y = [dot(f[1], v, NN).astype(BF16) for v in y]
        gate = [0.5 + 0.5 * jnp.tanh(gv[l, 0, c] * v.astype(F32) + gv[l, 1, c]) for c, v in zip(ids, u)]
        y = [(dot(v, h[1], NT) * q).astype(BF16) for v, q in zip(y, gate)]
        y = [dot(v, f[2], NT).astype(BF16) for v in y]
        y = [(dot(h[2], v, NN) * kt[l, 1]).astype(BF16) for v in y]
        y = [dot(f[3], v, NN).astype(BF16) for v in y]
        for c, v, base in zip(ids, y, u):
            store(c, base.astype(F32) + dot(v, h[3], NT))

    for d in range(1, half):
        ks_copy(d, lax.rem(s + n - 2 * d, n)).wait_recv()
        kf_copy(d, lax.rem(s + n - 2 * d, n)).start()
    for d in range(half):
        kf_copy(d, lax.rem(sib + n - 2 * d, n)).wait_recv()
    lax.fori_loop(0, layers, prepare, 0)

    def step(l, g):
        @pl.when(l == 0)
        def _():
            def arrive(d, _):
                in_wait(g, d)
                return 0

            lax.fori_loop(1, n, arrive, 0)

        compute(l, g)

        @pl.when(l == layers - 1)
        def _():
            def leave(d, _):
                out_copy(g, d).start()
                return 0

            lax.fori_loop(1, n, leave, 0)
            here = pl.ds(g * group, group)
            pltpu.make_async_copy(x.at[here, s], out.at[s, here], out_own.at[g]).start()

    per = maps // groups if maps % groups == 0 else maps
    whole = max(layers - 3, 1)

    def layer(l, _):
        sib_arrive(l)

        def one(g, _):
            step(l, g)

            @pl.when(jnp.logical_and(l + 1 < nz - 1, g * per < maps))
            def _():
                for j in range(per):
                    stage(l + 1, g * per + j)

            return 0

        lax.fori_loop(0, groups, one, 0)

        return 0

    lax.fori_loop(0, whole, layer, 0)

    def last(g, _):
        def one(l, _):
            @pl.when(jnp.logical_and(g == 0, jnp.logical_and(l > whole, l < nz - 1)))
            def _():
                for i in range(maps):
                    stage(l, i)

            @pl.when(g == 0)
            def _():
                sib_arrive(l)

            step(l, g)
            return 0

        return lax.fori_loop(whole, layers, one, 0)

    lax.fori_loop(0, groups, last, 0)

    def drain_group(g, _):
        def one(d, _):
            in_copy(g, d).wait_send()
            out_copy(g, d).wait_send()
            out_wait(g, d)
            return 0

        lax.fori_loop(1, n, one, 0)
        here = pl.ds(g * group, group)
        pltpu.make_async_copy(x.at[here, s], out.at[s, here], out_own.at[g]).wait()
        return 0

    lax.fori_loop(0, groups, drain_group, 0)

    for d in range(1, nz):
        for c in kz_copy(d, z):
            c.wait_send()
    for d in range(1, half):
        ks_copy(d, s).wait_send()
    for d in range(half):
        kf_copy(d, lax.rem(s + n - 2 * d, n)).wait_send()

    def drain_layer(l, _):
        @pl.when(z != l)
        def _():
            for r in range(maps):
                sib_copy(l, r).wait_send()

        @pl.when(jnp.logical_and(l <= z, z < nz - 1))
        def _():
            for r in range(maps):
                z_copy(l, r, True).wait_send()

        @pl.when(jnp.logical_and(l >= z, z > 0))
        def _():
            for r in range(maps):
                z_copy(l, r, False).wait_send()

        return 0

    lax.fori_loop(0, layers, drain_layer, 0)


def solution(mesh):
    n, nz = mesh.shape["seq"], mesh.shape["segment"]

    def local(sequence, first, second, kernels, scale, bias):
        rows, local_channels, radix = sequence.shape
        channels = local_channels // n
        group = min(4, channels)
        groups = channels // group
        maps = first.shape[1]
        layers = nz
        total = scale.shape[1]
        x_in = sequence.reshape(rows, n, channels, radix)
        sem = pltpu.SemaphoreType.DMA
        anywhere = pl.BlockSpec(memory_space=pl.ANY)
        result = pl.pallas_call(
            functools.partial(kernel, n, nz, group),
            out_shape=jax.ShapeDtypeStruct((n, channels, rows, radix), BF16),
            in_specs=[anywhere] * 6,
            out_specs=anywhere,
            scratch_shapes=[
                pltpu.VMEM((n, rows, channels, radix), BF16),
                pltpu.VMEM((n, channels, rows, radix), BF16),
                pltpu.VMEM((channels, n, rows, radix), BF16),
                pltpu.VMEM((2, layers, maps, radix, radix), BF16),
                pltpu.VMEM((n, layers, 2, rows, radix), BF16),
                pltpu.VMEM((layers, 1, total), F32),
                pltpu.VMEM((layers, 1, total), F32),
                pltpu.VMEM((layers, 2, radix, radix), F32),
                pltpu.VMEM((layers, 2, channels, 1, radix), F32),
                sem((5,)),
                sem((n,)),
                sem((groups, n)),
                sem((groups, n)),
                sem((groups, n)),
                sem((groups, n)),
                sem((groups,)),
                sem((layers, maps)),
                sem((layers, maps)),
                sem((layers, maps)),
                sem((layers, maps)),
                sem((layers, maps)),
                sem((nz,)),
                sem((nz,)),
                sem((nz,)),
                sem((nz,)),
                sem((nz,)),
                sem((nz,)),
                sem((n // 2,)),
                sem((n // 2,)),
                sem((n // 2,)),
                sem((n // 2,)),
            ],
            compiler_params=pltpu.CompilerParams(
                collective_id=0, has_side_effects=True, vmem_limit_bytes=56 * 2**20
            ),
        )(x_in, first, second, kernels, scale, bias)
        return result.reshape(local_channels, rows, radix).transpose(1, 0, 2)

    placed = (
        P("seq", "segment", None),
        P("segment", None, None, None),
        P("segment", None, None, None),
        P("segment", None, "seq", None),
        P("segment", None),
        P("segment", None),
    )
    return jax.shard_map(
        local, mesh=mesh, in_specs=placed, out_specs=P("seq", "segment", None), check_vma=False
    )
```

```python
import functools

import jax
import jax.numpy as jnp
from jax import lax
from jax.experimental import pallas as pl
from jax.experimental.pallas import tpu as pltpu
from jax.sharding import PartitionSpec as P

F32, BF16 = jnp.float32, jnp.bfloat16
NT = (((1,), (1,)), ((), ()))
NN = (((1,), (0,)), ((), ()))


def dot(a, b, dims):
    return lax.dot_general(a, b, dims, preferred_element_type=F32)


def kernel(
    n, nz, group, seq_in, f_own, g_own, k_own, scale_own, bias_own, out,
    raw, x_in, x, w, kk, scales, biases, kt, gv,
    own_sem, raw_sem, in_send, in_recv, out_send, out_recv, out_own,
    up_send, down_send, z_recv, sib_send, sib_recv,
    kz_send, kz_recv, gz_send, gz_recv, bz_send, bz_recv, ks_send, ks_recv, kf_send, kf_recv,
):
    s, z = lax.axis_index("seq"), lax.axis_index("segment")
    core = lax.rem(s, 2)
    sib = s + 1 - 2 * core
    channels, _, rows, radix = x.shape
    groups = channels // group
    maps = w.shape[2]
    layers = w.shape[1]
    half = n // 2

    def peer(d):
        return lax.rem(s + d, n)

    def remote(src, dst, send, recv, **where):
        return pltpu.make_async_remote_copy(
            src_ref=src, dst_ref=dst, send_sem=send, recv_sem=recv,
            device_id=where, device_id_type=pl.DeviceIdType.MESH,
        )

    def in_copy(g, d):
        t = peer(d)
        here = pl.ds(g * group, group)
        return remote(
            x_in.at[t, here], x.at[here, s], in_send.at[g, d], in_recv.at[g, d], seq=t
        )

    def out_copy(g, d):
        t = peer(d)
        here = pl.ds(g * group, group)
        return remote(
            x.at[here, t], out.at[s, here], out_send.at[g, d], out_recv.at[g, d], seq=t
        )

    def z_copy(l, i, up):
        v = w.at[core, l, i]
        sem = up_send if up else down_send
        return remote(v, v, sem.at[l, i], z_recv.at[l, i], segment=z + 1 if up else z - 1)

    def sib_copy(l, r):
        v = w.at[core, l, r]
        return remote(v, v, sib_send.at[l, r], sib_recv.at[l, r], seq=sib)

    def sib_wait(l, r):
        v = w.at[1 - core, l, r]
        remote(v, v, sib_send.at[l, r], sib_recv.at[l, r], seq=sib).wait_recv()

    def kz_copy(d, l):
        to = lax.rem(z + d, nz)
        return (
            remote(kk.at[s, l], kk.at[s, l], kz_send.at[d], kz_recv.at[d], segment=to),
            remote(scales.at[l], scales.at[l], gz_send.at[d], gz_recv.at[d], segment=to),
            remote(biases.at[l], biases.at[l], bz_send.at[d], bz_recv.at[d], segment=to),
        )

    def ks_copy(d, owner):
        v = kk.at[owner]
        return remote(v, v, ks_send.at[d], ks_recv.at[d], seq=lax.rem(s + 2 * d, n))

    def kf_copy(d, owner):
        v = kk.at[owner]
        return remote(v, v, kf_send.at[d], kf_recv.at[d], seq=sib)

    def in_wait(g, d):
        here = pl.ds(g * group, group)
        v = x.at[here, lax.rem(s + n - d, n)]
        remote(v, v, in_send.at[g, d], in_recv.at[g, d], seq=peer(d)).wait_recv()

    def out_wait(g, d):
        here = pl.ds(g * group, group)
        v = out.at[lax.rem(s + n - d, n), here]
        remote(v, v, out_send.at[g, d], out_recv.at[g, d], seq=peer(d)).wait_recv()

    own = [
        pltpu.make_async_copy(f_own.at[0], w.at[0, z], own_sem.at[0]),
        pltpu.make_async_copy(g_own.at[0], w.at[1, z], own_sem.at[1]),
        pltpu.make_async_copy(k_own.at[0], kk.at[s, z], own_sem.at[2]),
        pltpu.make_async_copy(scale_own, scales.at[z], own_sem.at[3]),
        pltpu.make_async_copy(bias_own, biases.at[z], own_sem.at[4]),
    ]
    def raw_copy(d):
        t = peer(d)
        return pltpu.make_async_copy(seq_in.at[:, t], raw.at[t], raw_sem.at[d])

    for c in own:
        c.start()
    for d in range(1, n + 1):
        raw_copy(d % n).start()

    barrier = pltpu.get_barrier_semaphore()
    mesh_id = pl.DeviceIdType.MESH

    def greet(d, _):
        pl.semaphore_signal(barrier, inc=1, device_id={"seq": peer(d)}, device_id_type=mesh_id)
        return 0

    lax.fori_loop(1, n, greet, 0)

    def greet_z(d, _):
        to = lax.rem(z + d, nz)
        pl.semaphore_signal(barrier, inc=1, device_id={"segment": to}, device_id_type=mesh_id)
        return 0

    lax.fori_loop(1, nz, greet_z, 0)
    pl.semaphore_wait(barrier, n + nz - 2)

    for c in own:
        c.wait()

    for d in range(1, nz):
        for c in kz_copy(d, z):
            c.start()

    def send_in(g, _):
        def one(d, _):
            in_copy(g, d).start()
            return 0

        return lax.fori_loop(1, n, one, 0)

    def turned(d):
        raw_copy(d).wait()
        v = raw[peer(d)]
        return jnp.swapaxes(v, 0, 1)

    def turn(d, _):
        x_in[peer(d)] = turned(d)

        @pl.when(d > 1)
        def _():
            in_copy(0, d - 1).start()

        return 0

    def send_own(up):
        for i in range(maps):
            z_copy(z, i, up).start()

    @pl.when(jnp.logical_and(z != 1, z < nz - 1))
    def _():
        send_own(True)

    @pl.when(z > 0)
    def _():
        send_own(False)

    lax.fori_loop(1, n, turn, 0)
    x[:, pl.ds(s, 1)] = turned(0)[:, None]
    in_copy(0, n - 1).start()

    for d in range(1, nz):
        for c in kz_copy(d, lax.rem(z + nz - d, nz)):
            c.wait_recv()
    for d in range(1, half):
        ks_copy(d, s).start()
    kf_copy(0, s).start()
    lax.fori_loop(1, groups, send_in, 0)

    def relay(l, i, up):
        c = z_copy(l, i, up)
        c.wait_recv()

        @pl.when((z < nz - 1) if up else (z > 0))
        def _():
            c.start()

        sib_copy(l, i).start()

    def rise(k, i):
        @pl.when(z > k)
        def _():
            relay(k, i, True)

    def fall(k, i):
        @pl.when(z + k + 1 < nz)
        def _():
            relay(z + k + 1, i, False)

    def stage(k, i):
        rise(k, i)
        fall(k, i)

    def sib_arrive(l):
        @pl.when(z != l)
        def _():
            for r in range(maps):
                sib_wait(l, r)

    for i in range(maps):
        stage(0, i)

    @pl.when(jnp.logical_and(z == 1, z < nz - 1))
    def _():
        send_own(True)

    def load(c):
        v = x[c]
        if rows % 16:
            v = v.astype(F32)
        return v.reshape(radix, radix).astype(BF16)

    def store(c, v):
        x[c] = v.reshape(n, rows, radix).astype(BF16)

    total = scales.shape[2]
    first_channel = (z * n + s) * channels

    def prepare(l, _):
        for i in range(2):
            full = kk[:, l, i].astype(F32).reshape(radix, radix)
            kt[l, i] = full.T
        pick = lax.broadcasted_iota(jnp.int32, (channels, total), 1) == (
            lax.broadcasted_iota(jnp.int32, (channels, total), 0) + first_channel
        )
        for i, values in enumerate((scales[l], biases[l])):
            col = jnp.sum(jnp.where(pick, values, 0.0), axis=1, keepdims=True)
            wide = jnp.broadcast_to(0.5 * col, (channels, radix))
            gv[l, i] = wide.reshape(channels, 1, radix)
        return 0

    def compute(l, g):
        ids = [g * group + i for i in range(group)]
        f = [w[0, l, r] for r in range(maps)]
        h = [w[1, l, r] for r in range(maps)]
        u = [load(c) for c in ids]
        y = [dot(v, f[0], NT).astype(BF16) for v in u]
        y = [(dot(h[0], v, NN) * kt[l, 0]).astype(BF16) for v in y]
        y = [dot(f[1], v, NN).astype(BF16) for v in y]
        gate = [0.5 + 0.5 * jnp.tanh(gv[l, 0, c] * v.astype(F32) + gv[l, 1, c]) for c, v in zip(ids, u)]
        y = [(dot(v, h[1], NT) * q).astype(BF16) for v, q in zip(y, gate)]
        y = [dot(v, f[2], NT).astype(BF16) for v in y]
        y = [(dot(h[2], v, NN) * kt[l, 1]).astype(BF16) for v in y]
        y = [dot(f[3], v, NN).astype(BF16) for v in y]
        for c, v, base in zip(ids, y, u):
            store(c, base.astype(F32) + dot(v, h[3], NT))

    for d in range(1, half):
        ks_copy(d, lax.rem(s + n - 2 * d, n)).wait_recv()
        kf_copy(d, lax.rem(s + n - 2 * d, n)).start()
    for d in range(half):
        kf_copy(d, lax.rem(sib + n - 2 * d, n)).wait_recv()
    lax.fori_loop(0, layers, prepare, 0)

    def step(l, g):
        @pl.when(l == 0)
        def _():
            def arrive(d, _):
                in_wait(g, d)
                return 0

            lax.fori_loop(1, n, arrive, 0)

        compute(l, g)

        @pl.when(l == layers - 1)
        def _():
            def leave(d, _):
                out_copy(g, d).start()
                return 0

            lax.fori_loop(1, n, leave, 0)
            here = pl.ds(g * group, group)
            pltpu.make_async_copy(x.at[here, s], out.at[s, here], out_own.at[g]).start()

    per = maps // groups if maps % groups == 0 else maps
    whole = max(layers - 3, 1)

    passes_on = jnp.logical_and(z > 0, z < nz - 1)

    def layer(l, _):
        @pl.when(jnp.logical_and(l + 1 < nz - 1, passes_on))
        def _():
            for i in range(maps):
                stage(l + 1, i)

        sib_arrive(l)

        def one(g, _):
            step(l, g)

            @pl.when(
                jnp.logical_and(
                    jnp.logical_and(l + 1 < nz - 1, g * per < maps), jnp.logical_not(passes_on)
                )
            )
            def _():
                for j in range(per):
                    stage(l + 1, g * per + j)

            return 0

        lax.fori_loop(0, groups, one, 0)

        return 0

    lax.fori_loop(0, whole, layer, 0)

    def last(g, _):
        def one(l, _):
            @pl.when(jnp.logical_and(g == 0, jnp.logical_and(l > whole, l < nz - 1)))
            def _():
                for i in range(maps):
                    rise(l, i)

            @pl.when(jnp.logical_and(g == 0, jnp.logical_and(l > whole + 1, l < nz)))
            def _():
                for i in range(maps):
                    fall(l - 1, i)

            @pl.when(g == 0)
            def _():
                sib_arrive(l)

            step(l, g)
            return 0

        return lax.fori_loop(whole, layers, one, 0)

    lax.fori_loop(0, groups, last, 0)

    def drain_group(g, _):
        def one(d, _):
            in_copy(g, d).wait_send()
            out_copy(g, d).wait_send()
            out_wait(g, d)
            return 0

        lax.fori_loop(1, n, one, 0)
        here = pl.ds(g * group, group)
        pltpu.make_async_copy(x.at[here, s], out.at[s, here], out_own.at[g]).wait()
        return 0

    lax.fori_loop(0, groups, drain_group, 0)

    for d in range(1, nz):
        for c in kz_copy(d, z):
            c.wait_send()
    for d in range(1, half):
        ks_copy(d, s).wait_send()
    for d in range(half):
        kf_copy(d, lax.rem(s + n - 2 * d, n)).wait_send()

    def drain_layer(l, _):
        @pl.when(z != l)
        def _():
            for r in range(maps):
                sib_copy(l, r).wait_send()

        @pl.when(jnp.logical_and(l <= z, z < nz - 1))
        def _():
            for r in range(maps):
                z_copy(l, r, True).wait_send()

        @pl.when(jnp.logical_and(l >= z, z > 0))
        def _():
            for r in range(maps):
                z_copy(l, r, False).wait_send()

        return 0

    lax.fori_loop(0, layers, drain_layer, 0)


def solution(mesh):
    n, nz = mesh.shape["seq"], mesh.shape["segment"]

    def local(sequence, first, second, kernels, scale, bias):
        rows, local_channels, radix = sequence.shape
        channels = local_channels // n
        group = min(4, channels)
        groups = channels // group
        maps = first.shape[1]
        layers = nz
        total = scale.shape[1]
        x_in = sequence.reshape(rows, n, channels, radix)
        sem = pltpu.SemaphoreType.DMA
        anywhere = pl.BlockSpec(memory_space=pl.ANY)
        result = pl.pallas_call(
            functools.partial(kernel, n, nz, group),
            out_shape=jax.ShapeDtypeStruct((n, channels, rows, radix), BF16),
            in_specs=[anywhere] * 6,
            out_specs=anywhere,
            scratch_shapes=[
                pltpu.VMEM((n, rows, channels, radix), BF16),
                pltpu.VMEM((n, channels, rows, radix), BF16),
                pltpu.VMEM((channels, n, rows, radix), BF16),
                pltpu.VMEM((2, layers, maps, radix, radix), BF16),
                pltpu.VMEM((n, layers, 2, rows, radix), BF16),
                pltpu.VMEM((layers, 1, total), F32),
                pltpu.VMEM((layers, 1, total), F32),
                pltpu.VMEM((layers, 2, radix, radix), F32),
                pltpu.VMEM((layers, 2, channels, 1, radix), F32),
                sem((5,)),
                sem((n,)),
                sem((groups, n)),
                sem((groups, n)),
                sem((groups, n)),
                sem((groups, n)),
                sem((groups,)),
                sem((layers, maps)),
                sem((layers, maps)),
                sem((layers, maps)),
                sem((layers, maps)),
                sem((layers, maps)),
                sem((nz,)),
                sem((nz,)),
                sem((nz,)),
                sem((nz,)),
                sem((nz,)),
                sem((nz,)),
                sem((n // 2,)),
                sem((n // 2,)),
                sem((n // 2,)),
                sem((n // 2,)),
            ],
            compiler_params=pltpu.CompilerParams(
                collective_id=0, has_side_effects=True, vmem_limit_bytes=56 * 2**20
            ),
        )(x_in, first, second, kernels, scale, bias)
        return result.reshape(local_channels, rows, radix).transpose(1, 0, 2)

    placed = (
        P("seq", "segment", None),
        P("segment", None, None, None),
        P("segment", None, None, None),
        P("segment", None, "seq", None),
        P("segment", None),
        P("segment", None),
    )
    return jax.shard_map(
        local, mesh=mesh, in_specs=placed, out_specs=P("seq", "segment", None), check_vma=False
    )
```
